256 devices in a mesh: seq: 32 (over y, z), chan: 8 (over x, core).
Axes of the slice: x: 4, y: 4, z: 8, core: 2. Of those that a mesh axis runs over, the one named last changes fastest.
Arguments:
- ssm_input: bfloat16 [16384, 8192], P('seq', 'chan'), may hold values from -6 to 6
- ssm_gate: bfloat16 [16384, 8192], P('seq', 'chan'), may hold values from -24 to 24
- state_write: bfloat16 [16384, 8, 128], P('seq', 'chan'), may hold values from -6 to 6
- state_read: bfloat16 [16384, 8, 128], P('seq', 'chan'), may hold values from -0.0078125 to 0.0078125
- step_size: float32 [16384, 128], P('seq', 'chan'), may hold values from 0.25 to 2
- decay_log: float32 [16384, 128], P('seq', 'chan'), may hold values from -1.7 to 0
- skip_gain: float32 [128], P('chan'), may hold values from 0.5 to 2
- norm_gain: float32 [8192], P('chan'), may hold values from 0.1 to 1.9
- sign_bits: int32 [8192], P('chan'), may hold values from 0 to 1
- weight_codes: bfloat16 [8192, 4096], P('chan'), may hold values from -8 to 7, as said below
- group_scales: float32 [64, 4096], P('chan'), may hold values from 0.0012 to 0.0048
Outputs:
- mixed_out: bfloat16 [16384, 4096], P('seq', 'chan')
The draws below stay inside these ranges and needn't reach their ends.
Inputs may be any that keep to these rules, and one draw needn't show every extreme that they name: `sign_bits`: 1 flips the sign of an inner channel before the rotation. `weight_codes`: whole numbers.
All inputs are finite; a program needn't handle non-finite values.
Results may differ from the reference program's by a relative error of at most 0.017.
Values may be sent and summed in bfloat16 or wider, within the bound.
No kernel may reach another device: no remote copies, remote signals or barrier semaphores. Data moves between devices by JAX's collectives and lax.ppermute only.
A program may use at most 128 MiB of HBM per device.

```python
import math
import jax
import jax.numpy as jnp
from jax import lax

D = 4096
HEADS = 128
HDIM = 64
NSTATE = 128
GROUPS = 8
SPAN = 256
QGROUP = 128
TOK_DEV = 512
INNER = 8192
BLOCK = 1024
SEQUENCE_TOKENS = 16384


def draw_ssm_gate(key, part):
    base_key, column_key, row_key = jax.random.split(key, 3)
    base_draw = jnp.clip(jax.random.normal(base_key, (SEQUENCE_TOKENS, INNER), jnp.float32), -4.0, 4.0)
    row_scale = jnp.exp(jax.random.uniform(row_key, (SEQUENCE_TOKENS, 1), jnp.float32, math.log(0.5), math.log(2.0)))
    column = jnp.exp(jax.random.uniform(column_key, (INNER,), jnp.float32, math.log(0.3), math.log(3.0)))
    values = base_draw * column * row_scale
    return jnp.clip(values, -24.0, 24.0).astype(jnp.bfloat16)


def draw_decay_log(key, part):
    fast_key, quick_key, slow_key, token_key, block_key, location_seed, amount_key = jax.random.split(key, 7)
    fast_share = 0.5
    fast_mask = jax.random.uniform(fast_key, (HEADS,), jnp.float32) < fast_share
    quick_rate = jnp.exp(jax.random.uniform(quick_key, (HEADS,), jnp.float32, math.log(0.02), math.log(0.035)))
    slow_rate = jnp.exp(jax.random.uniform(slow_key, (HEADS,), jnp.float32, math.log(0.1), math.log(0.6))) / SEQUENCE_TOKENS
    per_head_decay = jnp.where(fast_mask, quick_rate, slow_rate)
    token_multiplier = jnp.exp(jax.random.uniform(token_key, (SEQUENCE_TOKENS, HEADS), jnp.float32, math.log(0.5), math.log(2.0)))
    block_multiplier = jnp.exp(jax.random.uniform(block_key, (SEQUENCE_TOKENS // TOK_DEV, HEADS), jnp.float32, math.log(0.5), math.log(2.0)))
    block_multiplier = jnp.repeat(block_multiplier, TOK_DEV, axis=0)
    spike_location = jax.random.randint(location_seed, (3,), 0, SEQUENCE_TOKENS)
    total_amount = jax.random.uniform(amount_key, (3,), jnp.float32, 0.22, 0.5)
    spike_penalty = jnp.zeros((SEQUENCE_TOKENS,), jnp.float32).at[spike_location].add(total_amount)
    return -(per_head_decay[None, :] * token_multiplier * block_multiplier + spike_penalty[:, None])


def draw_weight_codes(key, part):
    return jax.random.randint(key, (INNER, D), -8, 8).astype(jnp.float32).astype(jnp.bfloat16)


def with_ends(entries, stream_key, least, top_value):
    place = [jax.random.randint(jax.random.fold_in(stream_key, axis), (), 0, length) for axis, length in enumerate(entries.shape)]
    widest = entries.shape.index(max(entries.shape))
    next_to = place[:widest] + [(place[widest] + 1) % entries.shape[widest]] + place[widest + 1:]
    return entries.at[tuple(place)].set(least).at[tuple(next_to)].set(top_value)


def level_of(rng, dims, shards, smallest, top_value):
    factor_of = 1.0
    for axis_at, parts in shards:
        draws = jax.random.uniform(jax.random.fold_in(jax.random.fold_in(rng, 6), axis_at), (parts,), jnp.float32, smallest / len(shards), top_value / len(shards))
        factor_of = factor_of * jnp.repeat(jnp.exp(draws), dims[axis_at] // parts).reshape((-1,) + (1,) * (len(dims) - 1 - axis_at))
    return factor_of


def centred(own_key, dims, deviation, most, shards=(), kind=jnp.bfloat16):
    drawn = jax.random.normal(own_key, dims, jnp.float32) * deviation
    if len(shards) > 0:
        drawn = level_of(own_key, dims, shards, -0.22, 0.18) * drawn
    return jnp.clip(drawn, min=-most, max=most).astype(kind)


def setup_inputs(seed: int = 0) -> dict:
    key_list = jax.random.split(jax.random.key(seed), 12)
    return {
        "ssm_input": centred(key_list[0], (SEQUENCE_TOKENS, INNER), 1.0, 6.0, ((0, 32), (1, 8))),
        "ssm_gate": draw_ssm_gate(jax.random.fold_in(key_list[11], 71), 0),
        "state_write": centred(key_list[2], (SEQUENCE_TOKENS, GROUPS, NSTATE), 1.0, 6.0, ((0, 32), (1, 8))),
        "state_read": centred(key_list[3], (SEQUENCE_TOKENS, GROUPS, NSTATE), (2.0 / (NSTATE * SEQUENCE_TOKENS) ** 0.5), 0.0078125, ((0, 32), (1, 8))),
        "step_size": jnp.clip(jnp.exp(math.log(2.0) - 2.0794415 * jax.random.uniform(key_list[4], (SEQUENCE_TOKENS, HEADS), jnp.float32) ** level_of(key_list[4], (SEQUENCE_TOKENS, HEADS), ((0, 32), (1, 8)), -0.2, 0.2)), 0.25, 2.0),
        "decay_log": draw_decay_log(jax.random.fold_in(key_list[11], 71), 0),
        "skip_gain": jnp.clip(jnp.exp(math.log(2.0) - 1.3862944 * jax.random.uniform(key_list[6], (HEADS,), jnp.float32) ** level_of(key_list[6], (HEADS,), ((0, 8),), -0.2, 0.2)), 0.5, 2.0),
        "norm_gain": jnp.clip(1.0 + 0.18 * jax.random.normal(key_list[7], (INNER,), jnp.float32), 0.1, 1.9),
        "sign_bits": with_ends(jax.random.randint(key_list[8], (INNER,), 0, 2), jax.random.fold_in(key_list[8], 1), 0, 1).astype(jnp.int32),
        "weight_codes": draw_weight_codes(jax.random.fold_in(key_list[11], 71), 0),
        "group_scales": jnp.clip(jnp.exp(math.log(0.0048) - 1.3862944 * jax.random.uniform(key_list[10], (INNER // QGROUP, D), jnp.float32) ** level_of(key_list[10], (INNER // QGROUP, D), ((0, 8),), -0.2, 0.2)), 0.0012, 0.0048),
    }


PRECISE = lax.Precision.HIGHEST

def parity_table(order_size):
    indices = jnp.arange(order_size, dtype=jnp.int32)
    common = indices[:, None] & indices[None, :]
    parity_sum = jnp.zeros((order_size, order_size), jnp.int32)
    for shift_by in range(order_size.bit_length() - 1):
        parity_sum = parity_sum + (common >> shift_by & 1)
    return (1 - 2 * (parity_sum % 2)).astype(jnp.float32)

def span_scan(state_now, inputs):
    drive_in, write_part, read_part, decay_part = inputs
    length = decay_part.shape[0]
    groups, per_group = (drive_in.shape[1], drive_in.shape[2])
    cum_grid = jnp.cumsum(decay_part, axis=0).reshape(length, groups, per_group)
    mask_low = jnp.arange(length)[:, None] >= jnp.arange(length)[None, :]
    by_head = jnp.transpose(cum_grid, (1, 2, 0))
    differ = by_head[:, :, :, None] - by_head[:, :, None, :]
    weights = jnp.where(mask_low, jnp.exp(jnp.where(mask_low, differ, 0.0)), 0.0)
    scores = jnp.einsum('tgn,sgn->gts', read_part, write_part, precision=PRECISE)
    mixing = weights * scores[:, None]
    within = jnp.einsum('gqts,sgqp->tgqp', mixing, drive_in, precision=PRECISE)
    carried_in = jnp.exp(cum_grid)[..., None] * jnp.einsum('tgn,gqnp->tgqp', read_part, state_now, precision=PRECISE)
    last_cum = cum_grid[-1]
    carry_weight = jnp.exp(last_cum[None] - cum_grid)
    new_state = jnp.exp(last_cum)[..., None, None] * state_now + jnp.einsum('sgn,sgqp->gqnp', write_part, carry_weight[..., None] * drive_in, precision=PRECISE)
    return (new_state, within + carried_in)

def reference(ssm_input, ssm_gate, state_write, state_read, step_size, decay_log, skip_gain, norm_gain, sign_bits, weight_codes, group_scales):
    token_count = ssm_input.shape[0]
    per_group = HEADS // GROUPS
    raw_input = ssm_input.astype(jnp.float32).reshape(token_count, GROUPS, per_group, HDIM)
    drive_in = raw_input * step_size.reshape(token_count, GROUPS, per_group)[..., None]
    blocks = token_count // SPAN
    inputs = (drive_in.reshape(blocks, SPAN, GROUPS, per_group, HDIM), state_write.astype(jnp.float32).reshape(blocks, SPAN, GROUPS, NSTATE), state_read.astype(jnp.float32).reshape(blocks, SPAN, GROUPS, NSTATE), decay_log.reshape(blocks, SPAN, HEADS))
    zero_state = jnp.zeros((GROUPS, per_group, NSTATE, HDIM), jnp.float32)
    final_state, outputs = lax.scan(span_scan, zero_state, inputs)
    ssm_out = outputs.reshape(token_count, GROUPS, per_group, HDIM) + raw_input * skip_gain.reshape(GROUPS, per_group)[:, :, None]
    gated_out = ssm_out.reshape(token_count, INNER) * jax.nn.silu(ssm_gate.astype(jnp.float32))
    grouped = gated_out.reshape(token_count, GROUPS, INNER // GROUPS)
    mean_square = lax.optimization_barrier(jnp.mean(grouped * grouped, axis=-1, keepdims=True))
    normed = ((grouped * lax.rsqrt(mean_square + 1e-05)).reshape(token_count, INNER) * norm_gain).astype(jnp.bfloat16)
    signed = normed * (1 - 2 * sign_bits).astype(jnp.bfloat16)
    local_table = parity_table(BLOCK).astype(jnp.bfloat16)
    local_rot = jnp.dot(signed.reshape(token_count * (INNER // BLOCK), BLOCK), local_table, preferred_element_type=jnp.float32).astype(jnp.bfloat16)
    cross_table = parity_table(INNER // BLOCK)
    mixed_blocks = jnp.einsum('hg,tgk->thk', cross_table, local_rot.astype(jnp.float32).reshape(token_count, INNER // BLOCK, BLOCK), precision=PRECISE)
    rotated = (mixed_blocks * (1.0 / math.sqrt(INNER))).astype(jnp.bfloat16).reshape(token_count, INNER)
    weight = (weight_codes.astype(jnp.float32) * jnp.repeat(group_scales, QGROUP, axis=0)).astype(jnp.bfloat16)
    total_sum = jnp.zeros((token_count, D), jnp.float32)
    for block_index in range(INNER // BLOCK):
        lower = block_index * BLOCK
        partial_value = jnp.dot(rotated[:, lower:lower + BLOCK], weight[lower:lower + BLOCK], preferred_element_type=jnp.float32).astype(jnp.bfloat16)
        total_sum = total_sum + lax.optimization_barrier(partial_value).astype(jnp.float32)
    return total_sum.astype(jnp.bfloat16)
```

```python
import math

import jax
import jax.numpy as jnp
import numpy as np
from jax import lax
from jax.experimental import pallas as pl
from jax.experimental.pallas import tpu as pltpu
from jax.sharding import PartitionSpec as P

HDIM = 64
NSTATE = 128
CHUNK = 128
QGROUP = 128
INNER = 8192
ROT = 256
EXACT = lax.Precision.HIGHEST
F32 = jnp.float32
BF16 = jnp.bfloat16


def hadamard(order):
    table = np.ones((1, 1), np.float32)
    while table.shape[0] < order:
        table = np.block([[table, table], [table, -table]])
    return table


def exact_dot(a, b):
    return jnp.dot(a, b, precision=EXACT, preferred_element_type=F32)


def fast_dot(a, b):
    return jnp.dot(a, b, preferred_element_type=F32)


def end_state(x_ref, step_ref, decay_ref, write_t_ref, expand_ref, state_ref, total_ref):
    rows = x_ref.shape[0]
    row = lax.broadcasted_iota(jnp.int32, (rows, rows), 0)
    col = lax.broadcasted_iota(jnp.int32, (rows, rows), 1)
    later = jnp.where(col > row, 1.0, 0.0).astype(F32)
    decay = decay_ref[...]
    factor = jnp.exp(exact_dot(later, decay)) * step_ref[...]
    drive = x_ref[...].astype(F32) * exact_dot(factor, expand_ref[...])
    state_ref[...] = fast_dot(write_t_ref[...], drive.astype(BF16)).astype(BF16)
    total = jnp.broadcast_to(jnp.exp(jnp.sum(decay, axis=0, keepdims=True)), (8, decay.shape[1]))
    total_ref[...] = exact_dot(total, expand_ref[...])


def span_prefix(part_ref, enter_ref):
    count, rows = enter_ref.shape[0], enter_ref.shape[1]
    running = jnp.zeros((rows, 128), F32)
    for i in range(count):
        enter_ref[i] = running.astype(BF16)
        if i + 1 < count:
            pair = part_ref[i, rows:, :].astype(F32)
            factor = pair[:8] + pair[8:]
            factor = jnp.concatenate([factor] * (rows // 8), axis=0)
            running = factor * running + part_ref[i, :rows, :].astype(F32)


def mixer(
    x_ref, gate_ref, write_ref, write_t_ref, read_ref, step_ref, step_t_ref, decay_ref,
    decay_t_ref, enter_ref, expand_ref, skip_ref, gain_ref, table_ref, out_ref, state_ref,
):
    @pl.when(pl.program_id(0) == 0)
    def _():
        state_ref[...] = enter_ref[...].astype(F32)

    row = lax.broadcasted_iota(jnp.int32, (CHUNK, CHUNK), 0)
    col = lax.broadcasted_iota(jnp.int32, (CHUNK, CHUNK), 1)
    mask = row >= col
    lower = jnp.where(mask, 1.0, 0.0).astype(F32)
    upper = jnp.where(row <= col, 1.0, 0.0).astype(F32)
    expand = expand_ref[...]
    cum = exact_dot(lower, decay_ref[...])
    cum_t = exact_dot(decay_t_ref[...], upper)
    step_t = step_t_ref[...]
    last = cum[CHUNK - 1 :, :]
    x = x_ref[...]
    read = read_ref[...]
    scores = lax.dot_general(
        read, write_ref[...], (((1,), (1,)), ((), ())), preferred_element_type=F32
    )
    lane = lax.broadcasted_iota(jnp.int32, (CHUNK, 128), 1)
    pieces = []
    for pair in range(x.shape[1] // 128):
        block = x[:, pair * 128 : (pair + 1) * 128]
        mixing = []
        for head in (2 * pair, 2 * pair + 1):
            differ = cum[:, head : head + 1] - cum_t[head : head + 1, :]
            weight = jnp.exp(jnp.where(mask, differ, -1e30))
            mixing.append((weight * (scores * step_t[head : head + 1, :])).astype(BF16))
        zero = jnp.zeros_like(block)
        stacked = jnp.concatenate(
            [jnp.where(lane < HDIM, block, zero), jnp.where(lane < HDIM, zero, block)], axis=0
        )
        pieces.append(fast_dot(jnp.concatenate(mixing, axis=1), stacked))
    within = jnp.concatenate(pieces, axis=1)
    state = state_ref[...]
    carried = fast_dot(read, state.astype(BF16)) * exact_dot(jnp.exp(cum), expand)
    raw = x.astype(F32)
    drive = raw * exact_dot(jnp.exp(last - cum) * step_ref[...], expand)
    keep = exact_dot(jnp.broadcast_to(jnp.exp(last), (8, last.shape[1])), expand)[:1, :]
    state_ref[...] = keep * state + fast_dot(write_t_ref[...], drive.astype(BF16))
    ssm_out = within + carried + raw * skip_ref[...]
    gate = gate_ref[...].astype(F32)
    gated = ssm_out * (gate / (1.0 + jnp.exp(-gate)))
    mean_square = jnp.mean(gated * gated, axis=-1, keepdims=True)
    signed = (gated * lax.rsqrt(mean_square + 1e-05) * gain_ref[...]).astype(BF16)
    table = table_ref[...]
    count = x.shape[1] // ROT
    parts = [fast_dot(signed[:, k * ROT : (k + 1) * ROT], table) for k in range(count)]
    stride = 1
    while stride < count:
        parts = [
            parts[k ^ stride] - parts[k] if k & stride else parts[k] + parts[k ^ stride]
            for k in range(count)
        ]
        stride *= 2
    for k in range(count):
        out_ref[:, k * ROT : (k + 1) * ROT] = parts[k].astype(BF16)


def on_device(
    ssm_input, ssm_gate, state_write, state_read, step_size, decay_log, skip_gain, norm_gain,
    sign_bits, weight_codes, group_scales,
):
    rows, width = ssm_input.shape
    heads = step_size.shape[1]
    spans = lax.axis_size("seq")
    chan_count = lax.axis_size("chan")
    chips = chan_count // 2
    place = lax.axis_index("chan")
    chip, core = place // 2, place % 2
    out_width = weight_codes.shape[1] // chips

    def shift(block, by):
        route = [
            (c * 2 + k, (c + by) % chips * 2 + k) for c in range(chips) for k in range(2)
        ]
        return lax.ppermute(block, "chan", route)

    def swap(block):
        return lax.ppermute(block, "chan", [(i, i ^ 1) for i in range(chan_count)])

    def weight_block(target):
        start = target * out_width
        codes = lax.dynamic_slice_in_dim(weight_codes, start, out_width, 1)
        scales = lax.dynamic_slice_in_dim(group_scales, start, out_width, 1)
        codes = codes.astype(F32).reshape(-1, QGROUP, out_width)
        return (codes * scales[:, None, :]).astype(BF16).reshape(-1, out_width)

    offsets = (0, 1, chips - 1, 2)
    weights = [weight_block(chip)]
    for by in offsets[1:]:
        weights.append(shift(weight_block((chip + by) % chips), by))

    write = state_write.reshape(rows, NSTATE)
    read = state_read.reshape(rows, NSTATE)
    write_t = write.T
    expand = jnp.asarray(np.repeat(np.eye(heads, dtype=np.float32), width // heads, axis=1))
    state, total = pl.pallas_call(
        end_state,
        out_shape=(
            jax.ShapeDtypeStruct((NSTATE, width), BF16),
            jax.ShapeDtypeStruct((8, width), F32),
        ),
        cost_estimate=pl.CostEstimate(
            flops=2 * rows * NSTATE * width, bytes_accessed=4 << 20, transcendentals=rows * heads
        ),
    )(ssm_input, step_size, decay_log, write_t, expand)
    slice_rows = NSTATE // spans * (width // 128)
    high = lax.reduce_precision(total[0], 8, 7)
    low = total[0] - high
    factor = jnp.concatenate([high.reshape(-1, 128), low.reshape(-1, 128)], axis=0).astype(BF16)
    payload = jnp.concatenate(
        [
            state.reshape(spans, slice_rows, 128),
            jnp.broadcast_to(factor[None], (spans,) + factor.shape),
        ],
        axis=1,
    )
    gathered = lax.all_to_all(payload, "seq", 0, 0, tiled=True)
    prefixes = pl.pallas_call(
        span_prefix, out_shape=jax.ShapeDtypeStruct((spans, slice_rows, 128), BF16)
    )(gathered)
    entering = lax.all_to_all(prefixes, "seq", 0, 0, tiled=True).reshape(NSTATE, width)

    gain = (norm_gain * (1 - 2 * sign_bits).astype(F32))[None, :]
    skip = jnp.repeat(skip_gain, width // heads)[None, :]
    table = jnp.asarray(hadamard(ROT)).astype(BF16)

    def whole(shape):
        return pl.BlockSpec(shape, lambda i: (0, 0))

    def by_row(cols):
        return pl.BlockSpec((CHUNK, cols), lambda i: (i, 0))

    def by_col(count):
        return pl.BlockSpec((count, CHUNK), lambda i: (0, i))

    local_rot = pl.pallas_call(
        mixer,
        grid=(rows // CHUNK,),
        in_specs=[
            by_row(width), by_row(width), by_row(NSTATE), by_col(NSTATE), by_row(NSTATE),
            by_row(heads), by_col(heads), by_row(heads), by_col(heads), whole((NSTATE, width)),
            whole((heads, width)), whole((1, width)), whole((1, width)), whole((ROT, ROT)),
        ],
        out_specs=by_row(width),
        out_shape=jax.ShapeDtypeStruct((rows, width), BF16),
        scratch_shapes=[pltpu.VMEM((NSTATE, width), F32)],
        cost_estimate=pl.CostEstimate(
            flops=8 * rows * NSTATE * width, bytes_accessed=4 << 20, transcendentals=rows * width
        ),
    )(
        ssm_input, ssm_gate, write, write_t, read, step_size, step_size.T, decay_log,
        decay_log.T, entering, expand, skip, gain, table,
    )

    other = swap(local_rot).astype(F32)
    mine = local_rot.astype(F32)
    rot = jnp.where(core == 1, other - mine, mine + other).astype(BF16)
    half = rows // 2
    from_left = shift(rot, 1)
    from_right = shift(rot, chips - 1)
    far = jnp.concatenate(
        [shift(from_left[:half], 1), shift(from_right[half:], chips - 1)], axis=0
    )
    blocks = [rot, from_left, from_right, far]

    scale = 1.0 / math.sqrt(INNER)
    sources = [(chip + chips - by) % chips for by in offsets]
    wide = [w.astype(F32) for w in weights]
    mixed = []
    for a in sources:
        signs = [
            (1 - 2 * (((a & b) ^ ((a & b) >> 1)) & 1)).astype(F32) * scale for b in sources
        ]
        mixed.append(sum(s * w for s, w in zip(signs, wide)).astype(BF16))
    mixed = lax.optimization_barrier(mixed)
    product = sum(fast_dot(r, w) for r, w in zip(blocks, mixed))
    keep_half = lax.dynamic_slice_in_dim(product, core * (out_width // 2), out_width // 2, 1)
    give_half = lax.dynamic_slice_in_dim(product, (1 - core) * (out_width // 2), out_width // 2, 1)
    return (keep_half + swap(give_half.astype(BF16)).astype(F32)).astype(BF16)


def solution(mesh):
    in_specs = (
        P("seq", "chan"), P("seq", "chan"), P("seq", "chan", None), P("seq", "chan", None),
        P("seq", "chan"), P("seq", "chan"), P("chan"), P("chan"), P("chan"), P("chan", None),
        P("chan", None),
    )
    return jax.shard_map(
        on_device, mesh=mesh, in_specs=in_specs, out_specs=P("seq", "chan"), check_vma=False
    )
```

```python
import math

import jax
import jax.numpy as jnp
import numpy as np
from jax import lax
from jax.experimental import pallas as pl
from jax.experimental.pallas import tpu as pltpu
from jax.sharding import PartitionSpec as P


HDIM = 64
NSTATE = 128
CHUNK = 128
QGROUP = 128
INNER = 8192
ROT = 256
DEPTH = 8
EXACT = lax.Precision.HIGHEST
F32 = jnp.float32
BF16 = jnp.bfloat16


def hadamard(order):
    table = np.ones((1, 1), np.float32)
    while table.shape[0] < order:
        table = np.block([[table, table], [table, -table]])
    return table


def exact_dot(a, b):
    return jnp.dot(a, b, precision=EXACT, preferred_element_type=F32)


def fast_dot(a, b):
    return jnp.dot(a, b, preferred_element_type=F32)


def end_state(x_ref, step_ref, decay_ref, write_t_ref, expand_ref, state_ref, total_ref):
    rows = x_ref.shape[0]
    row = lax.broadcasted_iota(jnp.int32, (rows, rows), 0)
    col = lax.broadcasted_iota(jnp.int32, (rows, rows), 1)
    later = jnp.where(col > row, 1.0, 0.0).astype(F32)
    decay = decay_ref[...]
    factor = jnp.exp(exact_dot(later, decay)) * step_ref[...]
    drive = x_ref[...].astype(F32) * exact_dot(factor, expand_ref[...])
    state_ref[...] = fast_dot(write_t_ref[...], drive.astype(BF16)).astype(BF16)
    total = jnp.broadcast_to(jnp.exp(jnp.sum(decay, axis=0, keepdims=True)), (8, decay.shape[1]))
    total_ref[...] = exact_dot(total, expand_ref[...])


def span_prefix(part_ref, enter_ref):
    count, rows = enter_ref.shape[0], enter_ref.shape[1]
    running = jnp.zeros((rows, 128), F32)
    for i in range(count):
        enter_ref[i] = running.astype(BF16)
        if i + 1 < count:
            pair = part_ref[i, rows:, :].astype(F32)
            factor = pair[:8] + pair[8:]
            factor = jnp.concatenate([factor] * (rows // 8), axis=0)
            running = factor * running + part_ref[i, :rows, :].astype(F32)


def mixer(
    x_ref, gate_ref, write_ref, write_t_ref, read_ref, step_ref, step_t_ref, decay_ref,
    decay_t_ref, enter_ref, expand_ref, skip_ref, gain_ref, table_ref, out_ref, state_ref,
):
    @pl.when(pl.program_id(0) == 0)
    def _():
        state_ref[...] = enter_ref[...].astype(F32)

    row = lax.broadcasted_iota(jnp.int32, (CHUNK, CHUNK), 0)
    col = lax.broadcasted_iota(jnp.int32, (CHUNK, CHUNK), 1)
    mask = row >= col
    lower = jnp.where(mask, 1.0, 0.0).astype(F32)
    upper = jnp.where(row <= col, 1.0, 0.0).astype(F32)
    expand = expand_ref[...]
    cum = exact_dot(lower, decay_ref[...])
    cum_t = exact_dot(decay_t_ref[...], upper)
    step_t = step_t_ref[...]
    last = cum[CHUNK - 1 :, :]
    x = x_ref[...]
    read = read_ref[...]
    scores = lax.dot_general(
        read, write_ref[...], (((1,), (1,)), ((), ())), preferred_element_type=F32
    )
    lane = lax.broadcasted_iota(jnp.int32, (CHUNK, 128), 1)
    pieces = []
    for pair in range(x.shape[1] // 128):
        block = x[:, pair * 128 : (pair + 1) * 128]
        mixing = []
        for head in (2 * pair, 2 * pair + 1):
            differ = cum[:, head : head + 1] - cum_t[head : head + 1, :]
            weight = jnp.exp(jnp.where(mask, differ, -1e30))
            mixing.append((weight * (scores * step_t[head : head + 1, :])).astype(BF16))
        zero = jnp.zeros_like(block)
        stacked = jnp.concatenate(
            [jnp.where(lane < HDIM, block, zero), jnp.where(lane < HDIM, zero, block)], axis=0
        )
        pieces.append(fast_dot(jnp.concatenate(mixing, axis=1), stacked))
    within = jnp.concatenate(pieces, axis=1)
    state = state_ref[...]
    carried = fast_dot(read, state.astype(BF16)) * exact_dot(jnp.exp(cum), expand)
    raw = x.astype(F32)
    drive = raw * exact_dot(jnp.exp(last - cum) * step_ref[...], expand)
    keep = exact_dot(jnp.broadcast_to(jnp.exp(last), (8, last.shape[1])), expand)[:1, :]
    state_ref[...] = keep * state + fast_dot(write_t_ref[...], drive.astype(BF16))
    ssm_out = within + carried + raw * skip_ref[...]
    gate = gate_ref[...].astype(F32)
    gated = ssm_out * (gate / (1.0 + jnp.exp(-gate)))
    mean_square = jnp.mean(gated * gated, axis=-1, keepdims=True)
    signed = (gated * lax.rsqrt(mean_square + 1e-05) * gain_ref[...]).astype(BF16)
    table = table_ref[...]
    count = x.shape[1] // ROT
    parts = [fast_dot(signed[:, k * ROT : (k + 1) * ROT], table) for k in range(count)]
    stride = 1
    while stride < count:
        parts = [
            parts[k ^ stride] - parts[k] if k & stride else parts[k] + parts[k ^ stride]
            for k in range(count)
        ]
        stride *= 2
    for k in range(count):
        out_ref[:, k * ROT : (k + 1) * ROT] = parts[k].astype(BF16)


def on_device(
    ssm_input, ssm_gate, state_write, state_read, step_size, decay_log, skip_gain, norm_gain,
    sign_bits, weight_codes, group_scales,
):
    rows, width = ssm_input.shape
    heads = step_size.shape[1]
    spans = lax.axis_size("seq")
    chan_count = lax.axis_size("chan")
    chips = chan_count // 2
    place = lax.axis_index("chan")
    chip, core = place // 2, place % 2
    out_width = weight_codes.shape[1] // chips

    def shift(block, by):
        route = [
            (c * 2 + k, (c + by) % chips * 2 + k) for c in range(chips) for k in range(2)
        ]
        return lax.ppermute(block, "chan", route)

    def swap(block):
        return lax.ppermute(block, "chan", [(i, i ^ 1) for i in range(chan_count)])

    def weight_block(target, row=0, count=weight_codes.shape[0]):
        start = target * out_width
        codes = lax.dynamic_slice(weight_codes, (row, start), (count, out_width))
        scales = lax.dynamic_slice(
            group_scales, (row // QGROUP, start), (count // QGROUP, out_width)
        )
        codes = codes.astype(F32).reshape(-1, QGROUP, out_width)
        return (codes * scales[:, None, :]).astype(BF16).reshape(-1, out_width)

    span = lax.axis_index("seq")
    pairings = {
        1: lambda s: (s & 1, s ^ 1),
        chips - 1: lambda s: (s // DEPTH & 1, s ^ DEPTH),
        2: lambda s: (
            s // DEPTH + 1 & 1,
            ((s // DEPTH + 1 ^ 1) - 1) % (spans // DEPTH) * DEPTH + s % DEPTH,
        ),
    }
    offsets = (0, 1, chips - 1, 2)
    half_rows = weight_codes.shape[0] // 2
    halves = {}
    for by in offsets[1:]:
        part = pairings[by](span)[0]
        block = weight_block((chip + by) % chips, part * half_rows, half_rows)
        halves[by] = shift(block, by)

    write = state_write.reshape(rows, NSTATE)
    read = state_read.reshape(rows, NSTATE)
    write_t = write.T
    expand = jnp.asarray(np.repeat(np.eye(heads, dtype=np.float32), width // heads, axis=1))
    state, total = pl.pallas_call(
        end_state,
        name="end_state",
        out_shape=(
            jax.ShapeDtypeStruct((NSTATE, width), BF16),
            jax.ShapeDtypeStruct((8, width), F32),
        ),
        cost_estimate=pl.CostEstimate(
            flops=2 * rows * NSTATE * width, bytes_accessed=4 << 20, transcendentals=rows * heads
        ),
    )(ssm_input, step_size, decay_log, write_t, expand)
    slice_rows = NSTATE // spans * (width // 128)
    high = lax.reduce_precision(total[0], 8, 7)
    low = total[0] - high
    factor = jnp.concatenate([high.reshape(-1, 128), low.reshape(-1, 128)], axis=0).astype(BF16)
    payload = jnp.concatenate(
        [
            state.reshape(spans, slice_rows, 128),
            jnp.broadcast_to(factor[None], (spans,) + factor.shape),
        ],
        axis=1,
    )
    gathered = lax.all_to_all(payload, "seq", 0, 0, tiled=True)
    prefixes = pl.pallas_call(
        span_prefix, out_shape=jax.ShapeDtypeStruct((spans, slice_rows, 128), BF16)
    )(gathered)
    entering = lax.all_to_all(prefixes, "seq", 0, 0, tiled=True).reshape(NSTATE, width)

    gain = (norm_gain * (1 - 2 * sign_bits).astype(F32))[None, :]
    skip = jnp.repeat(skip_gain, width // heads)[None, :]
    table = jnp.asarray(hadamard(ROT)).astype(BF16)

    def whole(shape):
        return pl.BlockSpec(shape, lambda i: (0, 0))

    def by_row(cols):
        return pl.BlockSpec((CHUNK, cols), lambda i: (i, 0))

    def by_col(count):
        return pl.BlockSpec((count, CHUNK), lambda i: (0, i))

    local_rot = pl.pallas_call(
        mixer,
        name="mixer",
        grid=(rows // CHUNK,),
        in_specs=[
            by_row(width), by_row(width), by_row(NSTATE), by_col(NSTATE), by_row(NSTATE),
            by_row(heads), by_col(heads), by_row(heads), by_col(heads), whole((NSTATE, width)),
            whole((heads, width)), whole((1, width)), whole((1, width)), whole((ROT, ROT)),
        ],
        out_specs=by_row(width),
        out_shape=jax.ShapeDtypeStruct((rows, width), BF16),
        scratch_shapes=[pltpu.VMEM((NSTATE, width), F32)],
        cost_estimate=pl.CostEstimate(
            flops=8 * rows * NSTATE * width, bytes_accessed=4 << 20, transcendentals=rows * width
        ),
    )(
        ssm_input, ssm_gate, write, write_t, read, step_size, step_size.T, decay_log,
        decay_log.T, entering, expand, skip, gain, table,
    )

    other = swap(local_rot).astype(F32)
    mine = local_rot.astype(F32)
    rot = jnp.where(core == 1, other - mine, mine + other).astype(BF16)
    half = rows // 2
    from_left = shift(rot, 1)
    from_right = shift(rot, chips - 1)
    far = jnp.concatenate(
        [shift(from_left[:half], 1), shift(from_right[half:], chips - 1)], axis=0
    )
    blocks = [rot, from_left, from_right, far]

    scale = 1.0 / math.sqrt(INNER)
    sources = [(chip + chips - by) % chips for by in offsets]
    own = weight_block(chip)
    tops, bottoms = [own[:half_rows]], [own[half_rows:]]
    for by in offsets[1:]:
        part = pairings[by](span)[0]
        route = [(i, pairings[by](i)[1]) for i in range(spans)]
        traded = lax.ppermute(halves[by], "seq", route)
        tops.append(jnp.where(part == 0, halves[by], traded))
        bottoms.append(jnp.where(part == 0, traded, halves[by]))
    mixed = []
    for a in sources:
        signs = [
            (1 - 2 * (((a & b) ^ ((a & b) >> 1)) & 1)).astype(F32) * scale for b in sources
        ]
        mixed.append(
            jnp.concatenate(
                [
                    sum(s * w.astype(F32) for s, w in zip(signs, side)).astype(BF16)
                    for side in (tops, bottoms)
                ],
                axis=0,
            )
        )
    mixed = lax.optimization_barrier(mixed)
    product = sum(fast_dot(r, w) for r, w in zip(blocks, mixed))
    keep_half = lax.dynamic_slice_in_dim(product, core * (out_width // 2), out_width // 2, 1)
    give_half = lax.dynamic_slice_in_dim(product, (1 - core) * (out_width // 2), out_width // 2, 1)
    return (keep_half + swap(give_half.astype(BF16)).astype(F32)).astype(BF16)


def solution(mesh):
    in_specs = (
        P("seq", "chan"), P("seq", "chan"), P("seq", "chan", None), P("seq", "chan", None),
        P("seq", "chan"), P("seq", "chan"), P("chan"), P("chan"), P("chan"), P("chan", None),
        P("chan", None),
    )

    return jax.shard_map(
        on_device, mesh=mesh, in_specs=in_specs, out_specs=P("seq", "chan"), check_vma=False
    )
```
